128 devices in a mesh: row: 16 (over x, y_lo, core), col: 8 (over z, y_hi).
Axes of the slice: x: 4, y: 4 (y_hi: 2, y_lo: 2; y = y_hi * 2 + y_lo), z: 4, core: 2. Of those that a mesh axis runs over, the one named last changes fastest.
Arguments:
- basis_values: bfloat16 [16, 8, 16, 128, 1024], P('row', 'col'), may hold values from -2 to 2
- potential: float32 [16, 8, 1024], P('row', 'col'), may hold values from -4 to 4
- task_pairs: int32 [16, 8, 128, 2], P('row', 'col'), may hold values from 0 to 15
- task_owner: int32 [16, 8, 128, 1], P('row', 'col'), may hold values from 0 to 127; in each aligned block of 128 rows (0 to 127, 128 to 255, ..., all dimensions but the last counted through in order) at most 2 rows name the same one
- task_slot: int32 [16, 8, 128], P('row', 'col'), may hold values from 0 to 31
- matrix_blocks: bfloat16 [16, 16, 16, 128, 128], P('row', 'col'), may hold values from -4 to 4
- matrix_columns: int32 [16, 16, 16], P('row', 'col'), may hold values from 0 to 15
Outputs:
- fock_blocks: bfloat16 [16, 16, 16, 128, 128], P('row', 'col')
- square_blocks: bfloat16 [16, 16, 16, 128, 128], P('row', 'col')
The draws below stay inside these ranges and needn't reach their ends.
Inputs may be any that keep to these rules, and one draw needn't show every extreme that they name: `task_owner`: among the 128 tasks of one device no owner is named more than 2 times, a bound that some block reaches.
All inputs are finite; a program needn't handle non-finite values.
Results may differ from the reference program's by a relative error of at most 0.0057.
Values may be sent and summed in bfloat16 or wider, within the bound.
No kernel may reach another device: no remote copies, remote signals or barrier semaphores. Data moves between devices by JAX's collectives and lax.ppermute only.
A program may use at most 192 MiB of HBM per device.

```python
import math
import jax
import jax.numpy as jnp
import numpy as np
from jax import lax

BLOCK = 128
CELL_ROWS = 16
LOCAL_BLOCKS = 16
POINTS = 1024
TASKS_DEV = 128
GRID = 16
TASK_CAP = 2
N_ROW = 16
N_COL = 8
DEVICES = 128


def draw_matrix_columns(key, part):
    offset_key = jax.random.fold_in(key, 11)
    noise_key = jax.random.fold_in(key, 12)
    pick_key = jax.random.fold_in(key, 13)
    offsets = jax.random.randint(offset_key, (GRID,), 0, CELL_ROWS, dtype=jnp.int32)
    rows_here = jnp.arange(CELL_ROWS, dtype=jnp.int32)
    aligned = (rows_here[None, None, :] + offsets[None, :, None] - offsets[:, None, None] + CELL_ROWS) % CELL_ROWS
    scattered = jax.random.randint(noise_key, (GRID, GRID, CELL_ROWS), 0, CELL_ROWS, dtype=jnp.int32)
    picker = jax.random.randint(pick_key, (GRID, GRID, CELL_ROWS), 0, 4, dtype=jnp.int32)
    return jnp.where(picker == 0, scattered, aligned).astype(jnp.int32)


def plant(result, key, smallest, largest):
    shape = result.shape
    index_at = [jax.random.randint(jax.random.fold_in(key, axis), (), 0, shape[axis]) for axis in range(len(shape))]
    result = result.at[tuple(index_at)].set(smallest)
    longest = shape.index(max(shape))
    index_at[longest] = (index_at[longest] + 1) % shape[longest]
    return result.at[tuple(index_at)].set(largest)


def level_of(stream_key, dims, cuts, least, high):
    loudness, own = 1.0, jax.random.fold_in(stream_key, 6)
    for position, parts in cuts:
        steps = jnp.exp(jax.random.uniform(jax.random.fold_in(own, position), (parts,), jnp.float32, least / len(cuts), high / len(cuts)))
        loudness = loudness * jnp.repeat(steps, dims[position] // parts).reshape([-1 if axis == position else 1 for axis in range(len(dims))])
    return loudness


def assign_block(key, own, number, rows, count, top, most, slope):
    sequence = jax.random.permutation(key, count)
    heavy_load, ordinary = portions_of(count, rows * top, most, slope, True), portions_of(count, rows * top, most, slope, False)
    places = jnp.arange(count)

    def named(lengths, rotation):
        used = int((lengths > 0).sum())
        fixed = max(1, used // 4)
        passed = fixed + (places - fixed + rotation * (used - fixed)) % max(1, count - fixed)
        return jnp.zeros((count,), jnp.int32).at[sequence[jnp.where(places < fixed, places, passed)]].set(jnp.asarray(lengths, jnp.int32))

    lengths = jnp.where(number % 4 == 0, named(heavy_load, number // 4), named(ordinary, number - number // 4 - 1))
    mixed = jax.random.permutation(jax.random.fold_in(own, 3), count)
    source_of, taker = mixed[0:count // 2 * 2:2], mixed[1:count // 2 * 2:2]
    margin = jnp.minimum(lengths[source_of] - 1, most - lengths[taker]) // 2
    margin = jnp.where((source_of == sequence[0]) | (taker == sequence[0]) | (lengths[taker] == 0), 0, jnp.maximum(margin, 0))
    passed = jax.random.randint(jax.random.fold_in(own, 4), (count // 2,), 0, 1 << 20) % (margin + 1)
    lengths = lengths.at[source_of].add(-passed).at[taker].add(passed)
    members = jnp.searchsorted(jnp.cumsum(lengths), jnp.arange(rows * top), side="right").astype(jnp.int32)
    table = members.reshape(top, rows).T
    table = table[jax.random.permutation(jax.random.fold_in(own, 1), rows)]
    rotation = jax.random.randint(jax.random.fold_in(own, 2), (rows, 1), 0, top)
    return jnp.take_along_axis(table, (jnp.arange(top)[None, :] + rotation) % top, axis=1)


def portions_of(count, total, bound, skew, full):
    portions = [(1 << 20) // math.isqrt(grade ** skew) + 1 for grade in range(1, count + 1)]
    largest = bound if full else min(bound, max(-(-total // count), total * portions[0] // sum(portions)))
    least = 1 if total - largest >= count - 1 else 0
    given, spare = [largest] + [least] * (count - 1), total - largest - least * (count - 1)
    while spare > 0:
        movable = [i for i in range(1, count) if given[i] < largest] or [i for i in range(1, count) if given[i] < bound]
        whole, budget = sum([portions[i] for i in movable]), spare
        for i in movable:
            extra = min(bound - given[i], max(1, budget * portions[i] // whole), spare)
            given[i] = given[i] + extra
            spare = spare - extra
    return np.array(given)


def scatter_about(own_key, extent, spread, bound, pieces=(), kind=jnp.bfloat16):
    entries = jax.random.normal(own_key, extent, jnp.float32) * spread
    if len(pieces) > 0:
        entries = level_of(own_key, extent, pieces, -0.22, 0.18) * entries
    return jnp.clip(entries, min=-bound, max=bound).astype(kind)


def setup_inputs(seed: int = 0) -> dict:
    key_of = jax.random.split(jax.random.key(seed), 8)
    basis_values = scatter_about(key_of[0], (N_ROW, N_COL, LOCAL_BLOCKS, BLOCK, POINTS), 0.15, 2.0, ((0, 16), (1, 8)))
    potential = scatter_about(key_of[1], (N_ROW, N_COL, POINTS), 1.0, 4.0, ((0, 16), (1, 8)), jnp.float32)
    task_pairs = plant(jax.random.randint(key_of[2], (N_ROW, N_COL, TASKS_DEV, 2), 0, LOCAL_BLOCKS), jax.random.fold_in(key_of[2], 1), 0, LOCAL_BLOCKS - 1).astype(jnp.int32)
    task_owner_keys = jax.random.split(jax.random.fold_in(key_of[3], 1), N_ROW * N_COL * TASKS_DEV // TASKS_DEV)
    task_owner_turns = jax.random.permutation(jax.random.fold_in(key_of[3], 3), N_ROW * N_COL * TASKS_DEV // TASKS_DEV)
    task_owner = jax.vmap(lambda own, number: assign_block(jax.random.fold_in(key_of[3], 2), own, number, TASKS_DEV, DEVICES, 1, TASK_CAP, 2))(task_owner_keys, task_owner_turns).reshape((N_ROW, N_COL, TASKS_DEV, 1))
    task_slot = plant(jax.random.randint(key_of[4], (N_ROW, N_COL, TASKS_DEV), 0, 2 * CELL_ROWS), jax.random.fold_in(key_of[4], 1), 0, (2 * CELL_ROWS) - 1).astype(jnp.int32)
    matrix_blocks = scatter_about(key_of[5], (GRID, GRID, CELL_ROWS, BLOCK, BLOCK), 0.3, 4.0, ((0, 16), (1, 8)))
    matrix_columns = draw_matrix_columns(jax.random.fold_in(key_of[7], 71), 0)
    return {"basis_values": basis_values, "potential": potential, "task_pairs": task_pairs, "task_owner": task_owner, "task_slot": task_slot, "matrix_blocks": matrix_blocks, "matrix_columns": matrix_columns}


def pair_blocks(device_basis, device_potential, device_pairs):
    weighted = (device_basis.astype(jnp.float32) * device_potential[None, None, :]).astype(jnp.bfloat16)
    left_rows = weighted[device_pairs[:, 0]].astype(jnp.float32)
    right_rows = device_basis[device_pairs[:, 1]].astype(jnp.float32)
    return jnp.einsum("tap,tbp->tab", left_rows, right_rows).astype(jnp.bfloat16)


def reference(basis_values, potential, task_pairs, task_owner, task_slot, matrix_blocks, matrix_columns):
    grid_size = matrix_blocks.shape[0]
    cell_rows = matrix_blocks.shape[2]
    block_width = matrix_blocks.shape[3]
    basis_flat = basis_values.reshape((-1,) + basis_values.shape[2:])
    potential_flat = potential.reshape((-1, potential.shape[-1]))
    pairs_flat = task_pairs.reshape((-1,) + task_pairs.shape[2:])
    targets = (task_owner[..., 0] * (2 * cell_rows) + task_slot).astype(jnp.int32)
    targets = targets.reshape((-1, task_slot.shape[-1]))
    fock_zero = jnp.zeros((grid_size * grid_size * cell_rows, block_width, block_width), jnp.float32)

    def add_device(fock_sum, inputs):
        device_basis, device_potential, device_pairs, device_targets = inputs
        blocks = pair_blocks(device_basis, device_potential, device_pairs)
        return fock_sum.at[device_targets].add(blocks.astype(jnp.float32)), None

    fock_sum, unused = lax.scan(add_device, fock_zero, (basis_flat, potential_flat, pairs_flat, targets))
    fock_blocks = fock_sum.reshape((grid_size, grid_size, cell_rows, block_width, block_width)).astype(jnp.bfloat16)

    cell_index = jnp.arange(grid_size, dtype=jnp.int32)

    def square_row(row_index):
        row_blocks = matrix_blocks[row_index].astype(jnp.float32)
        row_columns = matrix_columns[row_index]
        gathered = matrix_blocks[cell_index[:, None, None], cell_index[None, None, :], row_columns[:, :, None]]
        gathered_columns = matrix_columns[cell_index[:, None, None], cell_index[None, None, :], row_columns[:, :, None]]
        wanted = jnp.transpose(row_columns)[None, :, :]
        keep_mask = (gathered_columns == wanted).astype(jnp.float32)
        masked_terms = gathered.astype(jnp.float32) * keep_mask[..., None, None]
        return jnp.einsum("kqab,kqjbc->jqac", row_blocks, masked_terms)

    square_blocks = lax.map(square_row, cell_index).astype(jnp.bfloat16)
    return fock_blocks, square_blocks
```

```python
import functools

import jax
import jax.numpy as jnp
from jax import lax
from jax.experimental import pallas as pl
from jax.experimental.pallas import tpu as pltpu
from jax.sharding import Mesh
from jax.sharding import PartitionSpec as P

ROW = ("x", "yl", "c")
COL = ("z", "yh")
ALL = ROW + COL
F32 = jnp.float32
BF16 = jnp.bfloat16


def shift(value, axis, step):
    size = lax.axis_size(axis)
    return lax.ppermute(value, axis, [(i, (i + step) % size) for i in range(size)])


def pair_kernel(pairs, places, basis, potential, send, weighted, table, sem):
    local_count, width, points = basis.shape
    task_count = places.shape[0]
    for a in range(local_count):
        weighted[a] = (basis[a].astype(F32) * potential[...]).astype(BF16)

    def columns(step, carry):
        left = weighted[...].reshape(local_count * width, points)
        right = basis[pl.ds(2 * step, 2)].reshape(2 * width, points)
        product = lax.dot_general(left, right, (((1,), (1,)), ((), ())), preferred_element_type=F32)
        product = product.astype(BF16).reshape(local_count, width, 2 * width)
        table[2 * step] = product[:, :, :width]
        table[2 * step + 1] = product[:, :, width:]
        return carry

    lax.fori_loop(0, local_count // 2, columns, 0)

    def start(t, carry):
        block = table.at[pairs[2 * t + 1], pairs[2 * t]]
        pltpu.make_async_copy(block, send.at[places[t]], sem).start()
        return carry

    lax.fori_loop(0, task_count, start, 0)
    whole = send.at[pl.ds(0, task_count)]
    pltpu.make_async_copy(whole, whole, sem).wait()


def pair_blocks(basis, potential, pairs, places, slot_count):
    local_count, width, points = basis.shape
    task_count = places.shape[0]
    smem = pl.BlockSpec(memory_space=pltpu.SMEM)
    vmem = pl.BlockSpec(memory_space=pltpu.VMEM)
    return pl.pallas_call(
        pair_kernel,
        out_shape=jax.ShapeDtypeStruct((slot_count, width, width), BF16),
        in_specs=[smem, smem, vmem, vmem],
        out_specs=pl.BlockSpec(memory_space=pl.ANY),
        scratch_shapes=[
            pltpu.VMEM((local_count, width, points), BF16),
            pltpu.VMEM((local_count, local_count, width, width), BF16),
            pltpu.SemaphoreType.DMA,
        ],
        cost_estimate=pl.CostEstimate(
            flops=2 * (local_count * width) ** 2 * points,
            transcendentals=0,
            bytes_accessed=2 * basis.size + 2 * task_count * width * width,
        ),
        name="pair_blocks",
    )(pairs.reshape(-1), places, basis, potential)


def fock_kernel(slots, arrived, out, total):
    step = pl.program_id(0)
    chunk = arrived.shape[0]

    @pl.when(step == 0)
    def _():
        total[...] = jnp.zeros_like(total)

    def add(t, carry):
        slot = slots[step * chunk + t]

        @pl.when(slot >= 0)
        def _():
            total[slot] += arrived[t].astype(F32)

        return carry

    lax.fori_loop(0, chunk, add, 0)

    @pl.when(step == pl.num_programs(0) - 1)
    def _():
        out[...] = total[...].astype(BF16)


def fock_sum(slots, arrived, slot_count):
    count, width, _ = arrived.shape
    chunk = 32
    return pl.pallas_call(
        fock_kernel,
        grid=(count // chunk,),
        out_shape=jax.ShapeDtypeStruct((slot_count, width, width), BF16),
        in_specs=[
            pl.BlockSpec(memory_space=pltpu.SMEM),
            pl.BlockSpec((chunk, width, width), lambda s: (s, 0, 0)),
        ],
        out_specs=pl.BlockSpec((slot_count, width, width), lambda s: (0, 0, 0)),
        scratch_shapes=[pltpu.VMEM((slot_count, width, width), F32)],
        cost_estimate=pl.CostEstimate(
            flops=arrived.size, transcendentals=0, bytes_accessed=2 * arrived.size
        ),
        name="fock_sum",
    )(slots, arrived)


def square_kernel(places, cell_rows, where, picks, *refs):
    pieces = refs[: len(places)]
    out, left, right, sems = refs[len(places) :]
    cells = left.shape[0] // cell_rows
    width = left.shape[-1]
    zero = right.shape[0] - 1
    copies = []
    for n, (side, cell_count) in enumerate(places):
        size = cell_count * cell_rows
        first = pl.multiple_of(where[n], cell_rows)
        target = (left if side == 0 else right).at[pl.ds(first, size)]
        copies.append(pltpu.make_async_copy(pieces[n], target, sems.at[n]))
    for copy in copies:
        copy.start()
    right[zero] = jnp.zeros((width, width), BF16)
    for copy in copies:
        copy.wait()

    def block_row(q, carry):
        total = jnp.zeros((width, 2 * width), F32)
        for k in range(0, cells, 2):
            a = jnp.concatenate([left[k * cell_rows + q], left[(k + 1) * cell_rows + q]], axis=1)
            b = [[right[picks[(q * cells + k + h) * 2 + j]] for j in range(2)] for h in range(2)]
            b = jnp.concatenate([jnp.concatenate(b[h], axis=1) for h in range(2)], axis=0)
            total += jnp.dot(a, b, preferred_element_type=F32)
        out[q] = total[:, :width].astype(BF16)
        out[cell_rows + q] = total[:, width:].astype(BF16)
        return carry

    lax.fori_loop(0, cell_rows, block_row, 0)


def square_sum(picks, pieces, cells, cell_rows, width):
    places = tuple((side, piece.shape[0] // cell_rows) for side, _, piece in pieces)
    where = jnp.stack([first for _, first, _ in pieces]).astype(jnp.int32) * cell_rows
    smem = pl.BlockSpec(memory_space=pltpu.SMEM)
    return pl.pallas_call(
        functools.partial(square_kernel, places, cell_rows),
        out_shape=jax.ShapeDtypeStruct((2 * cell_rows, width, width), BF16),
        in_specs=[smem, smem] + [pl.BlockSpec(memory_space=pl.ANY)] * len(pieces),
        out_specs=pl.BlockSpec(memory_space=pltpu.VMEM),
        scratch_shapes=[
            pltpu.VMEM((cells * cell_rows, width, width), BF16),
            pltpu.VMEM((cells * 2 * cell_rows + 1, width, width), BF16),
            pltpu.SemaphoreType.DMA((len(pieces),)),
        ],
        cost_estimate=pl.CostEstimate(
            flops=4 * cells * cell_rows * width**3,
            transcendentals=0,
            bytes_accessed=2 * 3 * cells * cell_rows * width * width,
        ),
        name="square_sum",
    )(where, picks, *[piece for _, _, piece in pieces])


def ring_and_pair(own, ring, pair, half):
    got = {(0, 0): [(None, own)]}
    across = shift(own, pair, 1)
    got[(0, 1)] = [(None, across)]
    for other, value in ((0, own), (1, across)):
        behind, ahead = shift(value, ring, 1), shift(value, ring, -1)
        got[(3, other)] = [(None, behind)]
        got[(1, other)] = [(None, ahead)]
        got[(2, other)] = [
            (0, shift(behind[:half], ring, 1)),
            (1, shift(ahead[half:], ring, -1)),
        ]
    return got


def body(basis_values, potential, task_pairs, task_owner, task_slot, matrix_blocks, matrix_columns):
    x, yl, c, z, yh = (lax.axis_index(axis) for axis in ALL)
    cell_rows, width = matrix_blocks.shape[2], matrix_blocks.shape[3]
    row_count = lax.axis_size(ROW)
    device_count = row_count * lax.axis_size(COL)
    cells = 2 * lax.axis_size(COL)
    own = matrix_blocks.reshape(2 * cell_rows, width, width)

    rows = ring_and_pair(own, "z", "yh", cell_rows)
    columns = ring_and_pair(own, "x", "yl", cell_rows)
    pieces = []
    for (ring, pair), values in rows.items():
        first = 2 * (((z + ring) % 4) * 2 + (yh + pair) % 2)
        for half, value in values:
            pieces.append((0, first + (half or 0), value))
    for (ring, pair), values in columns.items():
        first = 2 * ((((x + ring) % 4) * 2 + (yl + pair) % 2) * 2 + c)
        other = 2 * ((((x + ring) % 4) * 2 + (yl + pair) % 2) * 2 + (1 - c))
        for half, value in values:
            pieces.append((1, first + (half or 0), value))
            pieces.append((1, other + (half or 0), shift(value, "c", 1)))

    owners, slots = task_owner.reshape(-1), task_slot.reshape(-1)
    task_count = owners.shape[0]
    order = jnp.arange(task_count, dtype=jnp.int32)
    earlier = (owners[:, None] == owners[None, :]) & (order[None, :] < order[:, None])
    places = owners * 2 + jnp.sum(earlier.astype(jnp.int32), axis=1)
    spots = jnp.arange(2 * device_count, dtype=jnp.int32)
    named = places[None, :] == spots[:, None]
    send_slots = jnp.max(jnp.where(named, slots[None, :], -1), axis=1)
    send = pair_blocks(basis_values[0, 0], potential[0], task_pairs[0, 0], places, 2 * device_count)

    own_columns = matrix_columns.reshape(1, -1)
    numbers = jnp.concatenate(
        [
            send_slots.reshape(device_count, 2),
            jnp.broadcast_to(own_columns, (device_count, own_columns.shape[1])),
        ],
        axis=1,
    )
    numbers = lax.all_to_all(numbers[:, None, :], ALL, 0, 0, tiled=True)[:, 0, :]
    arrived = lax.all_to_all(send, ALL, 0, 0, tiled=True)
    fock = fock_sum(numbers[:, :2].reshape(-1), arrived, 2 * cell_rows)

    every = numbers[:, 2:].reshape(row_count, cells, cell_rows)
    me_row = (x * 2 + yl) * 2 + c
    me_col = z * 2 + yh
    left_columns = lax.dynamic_index_in_dim(every, me_row, 0, keepdims=False)
    right_columns = lax.dynamic_slice_in_dim(every, 2 * me_col, 2, 1)
    target = matrix_columns.reshape(2, cell_rows)
    slot_range = jnp.arange(cell_rows, dtype=jnp.int32)
    cell_range = jnp.arange(cells, dtype=jnp.int32)
    chosen = left_columns.T[:, :, None, None] == slot_range
    found = jnp.sum(jnp.where(chosen, right_columns[None], 0), axis=-1)
    spot = (cell_range[None, :, None] * 2 + jnp.arange(2, dtype=jnp.int32)) * cell_rows
    spot = spot + left_columns.T[:, :, None]
    picks = jnp.where(found == target.T[:, None, :], spot, cells * 2 * cell_rows)
    square = square_sum(picks.reshape(-1), pieces, cells, cell_rows, width)
    shape = (1, 2, cell_rows, width, width)
    return fock.reshape(shape), square.reshape(shape)


def solution(mesh):
    finer = Mesh(mesh.devices.reshape(4, 2, 2, 4, 2), ALL)
    return jax.shard_map(
        body,
        mesh=finer,
        in_specs=(
            P(ROW, COL, None, None, None),
            P(ROW, COL, None),
            P(ROW, COL, None, None),
            P(ROW, COL, None, None),
            P(ROW, COL, None),
            P(ROW, COL, None, None, None),
            P(ROW, COL, None),
        ),
        out_specs=(P(ROW, COL, None, None, None), P(ROW, COL, None, None, None)),
        check_vma=False,
    )
```

```python
import functools

import jax
import jax.numpy as jnp
from jax import lax
from jax.experimental import pallas as pl
from jax.experimental.pallas import tpu as pltpu
from jax.sharding import Mesh
from jax.sharding import PartitionSpec as P

ROW = ("x", "yl", "c")
COL = ("z", "yh")
ALL = ROW + COL
F32 = jnp.float32
BF16 = jnp.bfloat16


def shift(value, axis, step):
    size = lax.axis_size(axis)
    return lax.ppermute(value, axis, [(i, (i + step) % size) for i in range(size)])


def pair_kernel(pairs, places, basis, potential, send, weighted, table, sem):
    local_count, width, points = basis.shape
    task_count = places.shape[0]
    for a in range(local_count):
        weighted[a] = (basis[a].astype(F32) * potential[...]).astype(BF16)

    def columns(step, carry):
        left = weighted[...].reshape(local_count * width, points)
        right = basis[pl.ds(2 * step, 2)].reshape(2 * width, points)
        product = lax.dot_general(left, right, (((1,), (1,)), ((), ())), preferred_element_type=F32)
        product = product.astype(BF16).reshape(local_count, width, 2 * width)
        table[2 * step] = product[:, :, :width]
        table[2 * step + 1] = product[:, :, width:]
        return carry

    lax.fori_loop(0, local_count // 2, columns, 0)

    def start(t, carry):
        block = table.at[pairs[2 * t + 1], pairs[2 * t]]
        pltpu.make_async_copy(block, send.at[places[t]], sem).start()
        return carry

    lax.fori_loop(0, task_count, start, 0)
    whole = send.at[pl.ds(0, task_count)]
    pltpu.make_async_copy(whole, whole, sem).wait()


def pair_blocks(basis, potential, pairs, places, slot_count):
    local_count, width, points = basis.shape
    task_count = places.shape[0]
    smem = pl.BlockSpec(memory_space=pltpu.SMEM)
    vmem = pl.BlockSpec(memory_space=pltpu.VMEM)
    return pl.pallas_call(
        pair_kernel,
        out_shape=jax.ShapeDtypeStruct((slot_count, width, width), BF16),
        in_specs=[smem, smem, vmem, vmem],
        out_specs=pl.BlockSpec(memory_space=pl.ANY),
        scratch_shapes=[
            pltpu.VMEM((local_count, width, points), BF16),
            pltpu.VMEM((local_count, local_count, width, width), BF16),
            pltpu.SemaphoreType.DMA,
        ],
        cost_estimate=pl.CostEstimate(
            flops=2 * (local_count * width) ** 2 * points,
            transcendentals=0,
            bytes_accessed=2 * basis.size + 2 * task_count * width * width,
        ),
        name="pair_blocks",
    )(pairs.reshape(-1), places, basis, potential)


def fock_kernel(slots, arrived, out, total):
    step = pl.program_id(0)
    chunk = arrived.shape[0]

    @pl.when(step == 0)
    def _():
        total[...] = jnp.zeros_like(total)

    def add(t, carry):
        slot = slots[step * chunk + t]

        @pl.when(slot >= 0)
        def _():
            total[slot] += arrived[t].astype(F32)

        return carry

    lax.fori_loop(0, chunk, add, 0)

    @pl.when(step == pl.num_programs(0) - 1)
    def _():
        out[...] = total[...].astype(BF16)


def fock_sum(slots, arrived, slot_count):
    count, width, _ = arrived.shape
    chunk = 32
    return pl.pallas_call(
        fock_kernel,
        grid=(count // chunk,),
        out_shape=jax.ShapeDtypeStruct((slot_count, width, width), BF16),
        in_specs=[
            pl.BlockSpec(memory_space=pltpu.SMEM),
            pl.BlockSpec((chunk, width, width), lambda s: (s, 0, 0)),
        ],
        out_specs=pl.BlockSpec((slot_count, width, width), lambda s: (0, 0, 0)),
        scratch_shapes=[pltpu.VMEM((slot_count, width, width), F32)],
        cost_estimate=pl.CostEstimate(
            flops=arrived.size, transcendentals=0, bytes_accessed=2 * arrived.size
        ),
        name="fock_sum",
    )(slots, arrived)


def square_kernel(places, cell_rows, where, picks, *refs):
    pieces = refs[: len(places)]
    out, left, right, sems = refs[len(places) :]
    cells = left.shape[0] // cell_rows
    width = left.shape[-1]
    zero = right.shape[0] - 1
    copies = []
    for n, (side, cell_count) in enumerate(places):
        size = cell_count * cell_rows
        first = pl.multiple_of(where[n], cell_rows)
        target = (left if side == 0 else right).at[pl.ds(first, size)]
        copies.append(pltpu.make_async_copy(pieces[n], target, sems.at[n]))
    for copy in copies:
        copy.start()
    right[zero] = jnp.zeros((width, width), BF16)
    for copy in copies:
        copy.wait()

    def block_row(q, carry):
        total = jnp.zeros((width, 2 * width), F32)
        for k in range(0, cells, 2):
            a = jnp.concatenate([left[k * cell_rows + q], left[(k + 1) * cell_rows + q]], axis=1)
            b = [[right[picks[(q * cells + k + h) * 2 + j]] for j in range(2)] for h in range(2)]
            b = jnp.concatenate([jnp.concatenate(b[h], axis=1) for h in range(2)], axis=0)
            total += jnp.dot(a, b, preferred_element_type=F32)
        out[q] = total[:, :width].astype(BF16)
        out[cell_rows + q] = total[:, width:].astype(BF16)
        return carry

    lax.fori_loop(0, cell_rows, block_row, 0)


def square_sum(picks, pieces, cells, cell_rows, width):
    places = tuple((side, piece.shape[0] // cell_rows) for side, _, piece in pieces)
    where = jnp.stack([first for _, first, _ in pieces]).astype(jnp.int32) * cell_rows
    smem = pl.BlockSpec(memory_space=pltpu.SMEM)
    return pl.pallas_call(
        functools.partial(square_kernel, places, cell_rows),
        out_shape=jax.ShapeDtypeStruct((2 * cell_rows, width, width), BF16),
        in_specs=[smem, smem] + [pl.BlockSpec(memory_space=pl.ANY)] * len(pieces),
        out_specs=pl.BlockSpec(memory_space=pltpu.VMEM),
        scratch_shapes=[
            pltpu.VMEM((cells * cell_rows, width, width), BF16),
            pltpu.VMEM((cells * 2 * cell_rows + 1, width, width), BF16),
            pltpu.SemaphoreType.DMA((len(pieces),)),
        ],
        cost_estimate=pl.CostEstimate(
            flops=4 * cells * cell_rows * width**3,
            transcendentals=0,
            bytes_accessed=2 * 3 * cells * cell_rows * width * width,
        ),
        name="square_sum",
    )(where, picks, *[piece for _, _, piece in pieces])


def first_wave(own, ring, pair):
    return [shift(own, ring, 1), shift(own, ring, -1), shift(own, pair, 1)]


def second_wave(first, ring, half):
    behind, ahead, across = first
    return [
        shift(across, ring, 1),
        shift(across, ring, -1),
        shift(behind[:half], ring, 1),
        shift(ahead[half:], ring, -1),
    ]


def third_wave(second, ring, half):
    return [shift(second[0][:half], ring, 1), shift(second[1][half:], ring, -1)]


def all_pieces(own, first, second, third):
    return {
        (0, 0): [(None, own)],
        (3, 0): [(None, first[0])],
        (1, 0): [(None, first[1])],
        (0, 1): [(None, first[2])],
        (3, 1): [(None, second[0])],
        (1, 1): [(None, second[1])],
        (2, 0): [(0, second[2]), (1, second[3])],
        (2, 1): [(0, third[0]), (1, third[1])],
    }


def body(basis_values, potential, task_pairs, task_owner, task_slot, matrix_blocks, matrix_columns):
    x, yl, c, z, yh = (lax.axis_index(axis) for axis in ALL)
    cell_rows, width = matrix_blocks.shape[2], matrix_blocks.shape[3]
    row_count = lax.axis_size(ROW)
    device_count = row_count * lax.axis_size(COL)
    cells = 2 * lax.axis_size(COL)
    own = matrix_blocks.reshape(2 * cell_rows, width, width)

    row_first = first_wave(own, "z", "yh")
    column_first = first_wave(own, "x", "yl")

    owners, slots = task_owner.reshape(-1), task_slot.reshape(-1)
    task_count = owners.shape[0]
    order = jnp.arange(task_count, dtype=jnp.int32)
    earlier = (owners[:, None] == owners[None, :]) & (order[None, :] < order[:, None])
    places = owners * 2 + jnp.sum(earlier.astype(jnp.int32), axis=1)
    spots = jnp.arange(2 * device_count, dtype=jnp.int32)
    named = places[None, :] == spots[:, None]
    send_slots = jnp.max(jnp.where(named, slots[None, :], -1), axis=1)
    send = pair_blocks(basis_values[0, 0], potential[0], task_pairs[0, 0], places, 2 * device_count)

    own_columns = matrix_columns.reshape(1, -1)
    numbers = jnp.concatenate(
        [
            send_slots.reshape(device_count, 2),
            jnp.broadcast_to(own_columns, (device_count, own_columns.shape[1])),
        ],
        axis=1,
    )
    numbers = lax.all_to_all(numbers[:, None, :], ALL, 0, 0, tiled=True)[:, 0, :]
    row_first, column_first, send, numbers = lax.optimization_barrier(
        (row_first, column_first, send, numbers)
    )
    row_second = second_wave(row_first, "z", cell_rows)
    column_second = second_wave(column_first, "x", cell_rows)
    row_second, column_second, send = lax.optimization_barrier((row_second, column_second, send))
    row_third = third_wave(row_second, "z", cell_rows)
    column_third = third_wave(column_second, "x", cell_rows)
    arrived = lax.all_to_all(send, ALL, 0, 0, tiled=True)
    fock = fock_sum(numbers[:, :2].reshape(-1), arrived, 2 * cell_rows)

    rows = all_pieces(own, row_first, row_second, row_third)
    columns = all_pieces(own, column_first, column_second, column_third)
    pieces = []
    for (ring, pair), values in rows.items():
        first = 2 * (((z + ring) % 4) * 2 + (yh + pair) % 2)
        for half, value in values:
            pieces.append((0, first + (half or 0), value))
    for (ring, pair), values in columns.items():
        first = 2 * ((((x + ring) % 4) * 2 + (yl + pair) % 2) * 2 + c)
        other = 2 * ((((x + ring) % 4) * 2 + (yl + pair) % 2) * 2 + (1 - c))
        for half, value in values:
            pieces.append((1, first + (half or 0), value))
            pieces.append((1, other + (half or 0), shift(value, "c", 1)))

    every = numbers[:, 2:].reshape(row_count, cells, cell_rows)
    me_row = (x * 2 + yl) * 2 + c
    me_col = z * 2 + yh
    left_columns = lax.dynamic_index_in_dim(every, me_row, 0, keepdims=False)
    right_columns = lax.dynamic_slice_in_dim(every, 2 * me_col, 2, 1)
    target = matrix_columns.reshape(2, cell_rows)
    slot_range = jnp.arange(cell_rows, dtype=jnp.int32)
    cell_range = jnp.arange(cells, dtype=jnp.int32)
    chosen = left_columns.T[:, :, None, None] == slot_range
    found = jnp.sum(jnp.where(chosen, right_columns[None], 0), axis=-1)
    spot = (cell_range[None, :, None] * 2 + jnp.arange(2, dtype=jnp.int32)) * cell_rows
    spot = spot + left_columns.T[:, :, None]
    picks = jnp.where(found == target.T[:, None, :], spot, cells * 2 * cell_rows)
    square = square_sum(picks.reshape(-1), pieces, cells, cell_rows, width)
    shape = (1, 2, cell_rows, width, width)
    return fock.reshape(shape), square.reshape(shape)


def solution(mesh):
    finer = Mesh(mesh.devices.reshape(4, 2, 2, 4, 2), ALL)
    return jax.shard_map(
        body,
        mesh=finer,
        in_specs=(
            P(ROW, COL, None, None, None),
            P(ROW, COL, None),
            P(ROW, COL, None, None),
            P(ROW, COL, None, None),
            P(ROW, COL, None),
            P(ROW, COL, None, None, None),
            P(ROW, COL, None),
        ),
        out_specs=(P(ROW, COL, None, None, None), P(ROW, COL, None, None, None)),
        check_vma=False,
    )
```

```python
import functools

import jax
import jax.numpy as jnp
from jax import lax
from jax.experimental import pallas as pl
from jax.experimental.pallas import tpu as pltpu
from jax.sharding import Mesh
from jax.sharding import PartitionSpec as P

ROW = ("x", "yl", "c")
COL = ("z", "yh")
ALL = ROW + COL
F32 = jnp.float32
BF16 = jnp.bfloat16


def shift(value, axis, step):
    size = lax.axis_size(axis)
    return lax.ppermute(value, axis, [(i, (i + step) % size) for i in range(size)])


def pair_kernel(pairs, owners, ranks, basis, potential, send0, send1, weighted, table, sem):
    local_count, width, points = basis.shape
    task_count = owners.shape[0]
    for a in range(local_count):
        weighted[a] = (basis[a].astype(F32) * potential[...]).astype(BF16)

    def columns(step, carry):
        left = weighted[...].reshape(local_count * width, points)
        right = basis[pl.ds(2 * step, 2)].reshape(2 * width, points)
        product = lax.dot_general(left, right, (((1,), (1,)), ((), ())), preferred_element_type=F32)
        product = product.astype(BF16).reshape(local_count, width, 2 * width)
        table[2 * step] = product[:, :, :width]
        table[2 * step + 1] = product[:, :, width:]
        return carry

    lax.fori_loop(0, local_count // 2, columns, 0)

    def start(t, carry):
        block = table.at[pairs[2 * t + 1], pairs[2 * t]]

        @pl.when(ranks[t] == 0)
        def _():
            pltpu.make_async_copy(block, send0.at[owners[t]], sem).start()

        @pl.when(ranks[t] != 0)
        def _():
            pltpu.make_async_copy(block, send1.at[owners[t]], sem).start()

        return carry

    lax.fori_loop(0, task_count, start, 0)
    whole = send0.at[pl.ds(0, task_count)]
    pltpu.make_async_copy(whole, whole, sem).wait()


def pair_blocks(basis, potential, pairs, owners, ranks, device_count):
    local_count, width, points = basis.shape
    task_count = owners.shape[0]
    smem = pl.BlockSpec(memory_space=pltpu.SMEM)
    vmem = pl.BlockSpec(memory_space=pltpu.VMEM)
    return pl.pallas_call(
        pair_kernel,
        out_shape=[jax.ShapeDtypeStruct((device_count, width, width), BF16)] * 2,
        in_specs=[smem, smem, smem, vmem, vmem],
        out_specs=[pl.BlockSpec(memory_space=pl.ANY)] * 2,
        scratch_shapes=[
            pltpu.VMEM((local_count, width, points), BF16),
            pltpu.VMEM((local_count, local_count, width, width), BF16),
            pltpu.SemaphoreType.DMA,
        ],
        cost_estimate=pl.CostEstimate(
            flops=2 * (local_count * width) ** 2 * points,
            transcendentals=0,
            bytes_accessed=2 * basis.size + 2 * task_count * width * width,
        ),
        name="pair_blocks",
    )(pairs.reshape(-1), owners, ranks, basis, potential)


def fock_kernel(order, starts, *refs):
    *before, arrived, out = refs

    def one_slot(slot, carry):
        if before:
            total = before[0][slot]
        else:
            total = jnp.zeros(out.shape[1:], F32)

        def add(p, total):
            return total + arrived[order[p]].astype(F32)

        total = lax.fori_loop(starts[slot], starts[slot + 1], add, total)
        out[slot] = total.astype(out.dtype)
        return carry

    lax.fori_loop(0, out.shape[0], one_slot, 0)


def fock_sum(slots, before, arrived, slot_count, kind):
    count, width, _ = arrived.shape
    number = jnp.arange(count, dtype=jnp.int32)
    valid = slots >= 0
    same = slots[None, :] == slots[:, None]
    ahead = (slots[None, :] < slots[:, None]) | (same & (number[None, :] < number[:, None]))
    spot = jnp.sum((ahead & valid[None, :]).astype(jnp.int32), axis=1)
    hit = (spot[None, :] == number[:, None]) & valid[None, :]
    order = jnp.sum(jnp.where(hit, number[None, :], 0), axis=1)
    bounds = jnp.arange(slot_count + 1, dtype=jnp.int32)
    starts = jnp.sum((valid & (slots < bounds[:, None])).astype(jnp.int32), axis=1)
    smem = pl.BlockSpec(memory_space=pltpu.SMEM)
    vmem = pl.BlockSpec(memory_space=pltpu.VMEM)
    return pl.pallas_call(
        fock_kernel,
        out_shape=jax.ShapeDtypeStruct((slot_count, width, width), kind),
        in_specs=[smem, smem] + [vmem] * (len(before) + 1),
        out_specs=vmem,
        cost_estimate=pl.CostEstimate(
            flops=arrived.size, transcendentals=0, bytes_accessed=2 * arrived.size
        ),
        name="fock_sum",
    )(order, starts, *before, arrived)


def square_kernel(places, cell_rows, where, picks, *refs):
    *pieces, out, left, right, sems = refs
    cells = left.shape[0] // cell_rows
    width = left.shape[-1]
    zero = right.shape[0] - 1
    copies = []
    for n, (piece, side, start, count) in enumerate(places):
        source = pieces[piece].at[pl.ds(start * cell_rows, count * cell_rows)]
        first = pl.multiple_of(where[n], cell_rows)
        target = (left if side == 0 else right).at[pl.ds(first, count * cell_rows)]
        copies.append(pltpu.make_async_copy(source, target, sems.at[n]))
    for copy in copies:
        copy.start()
    right[zero] = jnp.zeros((width, width), BF16)
    for copy in copies:
        copy.wait()

    def block_row(q, carry):
        total = jnp.zeros((width, 2 * width), F32)
        for k in range(0, cells, 2):
            a = jnp.concatenate([left[k * cell_rows + q], left[(k + 1) * cell_rows + q]], axis=1)
            b = [[right[picks[(q * cells + k + h) * 2 + j]] for j in range(2)] for h in range(2)]
            b = jnp.concatenate([jnp.concatenate(b[h], axis=1) for h in range(2)], axis=0)
            total += jnp.dot(a, b, preferred_element_type=F32)
        out[q] = total[:, :width].astype(BF16)
        out[cell_rows + q] = total[:, width:].astype(BF16)
        return carry

    lax.fori_loop(0, cell_rows, block_row, 0)


def square_sum(picks, parts, cells, cell_rows, width):
    pieces = []
    places = []
    for side, value, start, count, first in parts:
        if not any(value is piece for piece in pieces):
            pieces.append(value)
        index = [value is piece for piece in pieces].index(True)
        places.append((index, side, start, count))
    where = jnp.stack([part[4] for part in parts]).astype(jnp.int32) * cell_rows
    smem = pl.BlockSpec(memory_space=pltpu.SMEM)
    return pl.pallas_call(
        functools.partial(square_kernel, tuple(places), cell_rows),
        out_shape=jax.ShapeDtypeStruct((2 * cell_rows, width, width), BF16),
        in_specs=[smem, smem] + [pl.BlockSpec(memory_space=pl.ANY)] * len(pieces),
        out_specs=pl.BlockSpec(memory_space=pltpu.VMEM),
        scratch_shapes=[
            pltpu.VMEM((cells * cell_rows, width, width), BF16),
            pltpu.VMEM((cells * 2 * cell_rows + 1, width, width), BF16),
            pltpu.SemaphoreType.DMA((len(places),)),
        ],
        cost_estimate=pl.CostEstimate(
            flops=4 * cells * cell_rows * width**3,
            transcendentals=0,
            bytes_accessed=2 * 3 * cells * cell_rows * width * width,
        ),
        name="square_sum",
    )(where, picks, *pieces)


def body(basis_values, potential, task_pairs, task_owner, task_slot, matrix_blocks, matrix_columns):
    x, yl, c, z, yh = (lax.axis_index(axis) for axis in ALL)
    cell_rows, width = matrix_blocks.shape[2], matrix_blocks.shape[3]
    row_count = lax.axis_size(ROW)
    device_count = row_count * lax.axis_size(COL)
    cells = 2 * lax.axis_size(COL)
    half = cell_rows
    own = matrix_blocks.reshape(2 * cell_rows, width, width)

    x_behind, x_ahead = shift(own, "x", 1), shift(own, "x", -1)
    z_behind, z_ahead = shift(own, "z", 1), shift(own, "z", -1)
    y_low = shift(own, "yl", 1)
    y_both = lax.all_to_all(jnp.concatenate([own, own]), "yh", 0, 0, tiled=True)

    x_behind, x_ahead, z_behind, z_ahead, y_low, y_both, basis = lax.optimization_barrier(
        (x_behind, x_ahead, z_behind, z_ahead, y_low, y_both, basis_values)
    )
    y_high = lax.dynamic_slice_in_dim(y_both, (1 - yh) * 2 * cell_rows, 2 * cell_rows, 0)
    x_behind2, x_ahead2 = shift(y_low, "x", 1), shift(y_low, "x", -1)
    z_behind2, z_ahead2 = shift(y_high, "z", 1), shift(y_high, "z", -1)

    owners, slots = task_owner.reshape(-1), task_slot.reshape(-1)
    task_count = owners.shape[0]
    number = jnp.arange(task_count, dtype=jnp.int32)
    earlier = (owners[:, None] == owners[None, :]) & (number[None, :] < number[:, None])
    ranks = jnp.sum(earlier.astype(jnp.int32), axis=1)
    send0, send1 = pair_blocks(
        basis[0, 0], potential[0], task_pairs[0, 0], owners, ranks, device_count
    )
    spots = jnp.arange(device_count, dtype=jnp.int32)
    named = owners[None, :] == spots[:, None]
    send_slots = [
        jnp.max(jnp.where(named & (ranks == rank)[None, :], slots[None, :], -1), axis=1)
        for rank in range(2)
    ]
    own_columns = matrix_columns.reshape(1, -1)
    numbers = jnp.concatenate(
        [
            send_slots[0][:, None],
            send_slots[1][:, None],
            jnp.broadcast_to(own_columns, (device_count, own_columns.shape[1])),
        ],
        axis=1,
    )

    x_behind2, x_ahead2, z_behind2, z_ahead2, own2, x_behind, x_ahead, y_low, send0 = (
        lax.optimization_barrier(
            (x_behind2, x_ahead2, z_behind2, z_ahead2, own, x_behind, x_ahead, y_low, send0)
        )
    )
    arrived0 = lax.all_to_all(send0, ALL, 0, 0, tiled=True)
    x_far0 = shift(jnp.concatenate([x_behind[:half], x_behind2[:half]]), "x", 1)
    x_far1 = shift(jnp.concatenate([x_ahead[half:], x_ahead2[half:]]), "x", -1)
    z_far0 = shift(jnp.concatenate([z_behind[:half], z_behind2[:half]]), "z", 1)
    z_far1 = shift(jnp.concatenate([z_ahead[half:], z_ahead2[half:]]), "z", -1)

    arrived0, numbers = lax.optimization_barrier((arrived0, numbers))
    numbers = lax.all_to_all(numbers[:, None, :], ALL, 0, 0, tiled=True)[:, 0, :]
    x_far0, x_far1, z_far0, z_far1, numbers, send1 = lax.optimization_barrier(
        (x_far0, x_far1, z_far0, z_far1, numbers, send1)
    )
    arrived1 = lax.all_to_all(send1, ALL, 0, 0, tiled=True)

    parts = []

    def left(value, start, count, ring, pair, cell):
        first = 2 * (((z + ring) % 4) * 2 + (yh + pair) % 2) + cell
        parts.append((0, value, start, count, first))

    def right(value, *pieces):
        other = shift(value, "c", 1)
        for start, count, ring, pair, cell in pieces:
            base = 2 * (((x + ring) % 4) * 2 + (yl + pair) % 2)
            parts.append((1, value, start, count, 2 * (base // 2 * 2 + c) + cell))
            parts.append((1, other, start, count, 2 * (base // 2 * 2 + 1 - c) + cell))

    left(own, 0, 2, 0, 0, 0)
    left(z_behind, 0, 2, 3, 0, 0)
    left(z_ahead, 0, 2, 1, 0, 0)
    left(y_high, 0, 2, 0, 1, 0)
    left(z_behind2, 0, 2, 3, 1, 0)
    left(z_ahead2, 0, 2, 1, 1, 0)
    for pair in range(2):
        left(z_far0, pair, 1, 2, pair, 0)
        left(z_far1, pair, 1, 2, pair, 1)
    right(own2, (0, 2, 0, 0, 0))
    right(x_behind, (0, 2, 3, 0, 0))
    right(x_ahead, (0, 2, 1, 0, 0))
    right(y_low, (0, 2, 0, 1, 0))
    right(x_behind2, (0, 2, 3, 1, 0))
    right(x_ahead2, (0, 2, 1, 1, 0))
    right(x_far0, (0, 1, 2, 0, 0), (1, 1, 2, 1, 0))
    right(x_far1, (0, 1, 2, 0, 1), (1, 1, 2, 1, 1))

    every = numbers[:, 2:].reshape(row_count, cells, cell_rows)
    me_row = (x * 2 + yl) * 2 + c
    me_col = z * 2 + yh
    left_columns = lax.dynamic_index_in_dim(every, me_row, 0, keepdims=False)
    right_columns = lax.dynamic_slice_in_dim(every, 2 * me_col, 2, 1)
    target = matrix_columns.reshape(2, cell_rows)
    slot_range = jnp.arange(cell_rows, dtype=jnp.int32)
    cell_range = jnp.arange(cells, dtype=jnp.int32)
    chosen = left_columns.T[:, :, None, None] == slot_range
    found = jnp.sum(jnp.where(chosen, right_columns[None], 0), axis=-1)
    spot = (cell_range[None, :, None] * 2 + jnp.arange(2, dtype=jnp.int32)) * cell_rows
    spot = spot + left_columns.T[:, :, None]
    picks = jnp.where(found == target.T[:, None, :], spot, cells * 2 * cell_rows)
    square = square_sum(picks.reshape(-1), parts, cells, cell_rows, width)

    partial = fock_sum(numbers[:, 0], [], arrived0, 2 * cell_rows, F32)
    fock = fock_sum(numbers[:, 1], [partial], arrived1, 2 * cell_rows, BF16)
    shape = (1, 2, cell_rows, width, width)
    return fock.reshape(shape), square.reshape(shape)


def solution(mesh):
    finer = Mesh(mesh.devices.reshape(4, 2, 2, 4, 2), ALL)
    return jax.shard_map(
        body,
        mesh=finer,
        in_specs=(
            P(ROW, COL, None, None, None),
            P(ROW, COL, None),
            P(ROW, COL, None, None),
            P(ROW, COL, None, None),
            P(ROW, COL, None),
            P(ROW, COL, None, None, None),
            P(ROW, COL, None),
        ),
        out_specs=(P(ROW, COL, None, None, None), P(ROW, COL, None, None, None)),
        check_vma=False,
    )
```

```python
import functools

import jax
import jax.numpy as jnp
from jax import lax
from jax.experimental import pallas as pl
from jax.experimental.pallas import tpu as pltpu
from jax.sharding import Mesh
from jax.sharding import PartitionSpec as P

ROW = ("x", "yl", "c")
COL = ("z", "yh")
ALL = ROW + COL
F32 = jnp.float32
BF16 = jnp.bfloat16


def shift(value, axis, step):
    size = lax.axis_size(axis)
    return lax.ppermute(value, axis, [(i, (i + step) % size) for i in range(size)])


def pair_kernel(pairs, owners, ranks, basis, potential, send0, send1, weighted, table, sem):
    local_count, width, points = basis.shape
    task_count = owners.shape[0]
    for a in range(local_count):
        weighted[a] = (basis[a].astype(F32) * potential[...]).astype(BF16)

    def columns(step, carry):
        left = weighted[...].reshape(local_count * width, points)
        right = basis[pl.ds(2 * step, 2)].reshape(2 * width, points)
        product = lax.dot_general(left, right, (((1,), (1,)), ((), ())), preferred_element_type=F32)
        product = product.astype(BF16).reshape(local_count, width, 2 * width)
        table[2 * step] = product[:, :, :width]
        table[2 * step + 1] = product[:, :, width:]
        return carry

    lax.fori_loop(0, local_count // 2, columns, 0)

    def start(t, carry):
        block = table.at[pairs[2 * t + 1], pairs[2 * t]]

        @pl.when(ranks[t] == 0)
        def _():
            pltpu.make_async_copy(block, send0.at[owners[t]], sem).start()

        @pl.when(ranks[t] != 0)
        def _():
            pltpu.make_async_copy(block, send1.at[owners[t]], sem).start()

        return carry

    lax.fori_loop(0, task_count, start, 0)
    whole = send0.at[pl.ds(0, task_count)]
    pltpu.make_async_copy(whole, whole, sem).wait()


def pair_blocks(basis, potential, pairs, owners, ranks, device_count):
    local_count, width, points = basis.shape
    task_count = owners.shape[0]
    smem = pl.BlockSpec(memory_space=pltpu.SMEM)
    vmem = pl.BlockSpec(memory_space=pltpu.VMEM)
    return pl.pallas_call(
        pair_kernel,
        out_shape=[jax.ShapeDtypeStruct((device_count, width, width), BF16)] * 2,
        in_specs=[smem, smem, smem, vmem, vmem],
        out_specs=[pl.BlockSpec(memory_space=pl.ANY)] * 2,
        scratch_shapes=[
            pltpu.VMEM((local_count, width, points), BF16),
            pltpu.VMEM((local_count, local_count, width, width), BF16),
            pltpu.SemaphoreType.DMA,
        ],
        cost_estimate=pl.CostEstimate(
            flops=2 * (local_count * width) ** 2 * points,
            transcendentals=0,
            bytes_accessed=2 * basis.size + 2 * task_count * width * width,
        ),
        name="pair_blocks",
    )(pairs.reshape(-1), owners, ranks, basis, potential)


def fock_kernel(order, starts, *refs):
    *before, arrived, out = refs

    def one_slot(slot, carry):
        if before:
            total = before[0][slot]
        else:
            total = jnp.zeros(out.shape[1:], F32)

        def add(p, total):
            return total + arrived[order[p]].astype(F32)

        total = lax.fori_loop(starts[slot], starts[slot + 1], add, total)
        out[slot] = total.astype(out.dtype)
        return carry

    lax.fori_loop(0, out.shape[0], one_slot, 0)


def fock_sum(slots, before, arrived, slot_count, kind):
    count, width, _ = arrived.shape
    number = jnp.arange(count, dtype=jnp.int32)
    valid = slots >= 0
    same = slots[None, :] == slots[:, None]
    ahead = (slots[None, :] < slots[:, None]) | (same & (number[None, :] < number[:, None]))
    spot = jnp.sum((ahead & valid[None, :]).astype(jnp.int32), axis=1)
    hit = (spot[None, :] == number[:, None]) & valid[None, :]
    order = jnp.sum(jnp.where(hit, number[None, :], 0), axis=1)
    bounds = jnp.arange(slot_count + 1, dtype=jnp.int32)
    starts = jnp.sum((valid & (slots < bounds[:, None])).astype(jnp.int32), axis=1)
    smem = pl.BlockSpec(memory_space=pltpu.SMEM)
    vmem = pl.BlockSpec(memory_space=pltpu.VMEM)
    return pl.pallas_call(
        fock_kernel,
        out_shape=jax.ShapeDtypeStruct((slot_count, width, width), kind),
        in_specs=[smem, smem] + [vmem] * (len(before) + 1),
        out_specs=vmem,
        cost_estimate=pl.CostEstimate(
            flops=arrived.size, transcendentals=0, bytes_accessed=2 * arrived.size
        ),
        name="fock_sum",
    )(order, starts, *before, arrived)


def square_kernel(places, cell_rows, where, picks, *refs):
    *pieces, out, left, right, sems = refs
    cells = left.shape[0] // cell_rows
    width = left.shape[-1]
    zero = right.shape[0] - 1
    copies = []
    for n, (piece, side, start, count) in enumerate(places):
        source = pieces[piece].at[pl.ds(start * cell_rows, count * cell_rows)]
        first = pl.multiple_of(where[n], cell_rows)
        target = (left if side == 0 else right).at[pl.ds(first, count * cell_rows)]
        copies.append(pltpu.make_async_copy(source, target, sems.at[n]))
    for copy in copies:
        copy.start()
    right[zero] = jnp.zeros((width, width), BF16)
    for copy in copies:
        copy.wait()

    def block_row(q, carry):
        total = jnp.zeros((width, 2 * width), F32)
        for k in range(0, cells, 2):
            a = jnp.concatenate([left[k * cell_rows + q], left[(k + 1) * cell_rows + q]], axis=1)
            b = [[right[picks[(q * cells + k + h) * 2 + j]] for j in range(2)] for h in range(2)]
            b = jnp.concatenate([jnp.concatenate(b[h], axis=1) for h in range(2)], axis=0)
            total += jnp.dot(a, b, preferred_element_type=F32)
        out[q] = total[:, :width].astype(BF16)
        out[cell_rows + q] = total[:, width:].astype(BF16)
        return carry

    lax.fori_loop(0, cell_rows, block_row, 0)


def square_sum(picks, parts, cells, cell_rows, width):
    pieces = []
    places = []
    for side, value, start, count, first in parts:
        if not any(value is piece for piece in pieces):
            pieces.append(value)
        index = [value is piece for piece in pieces].index(True)
        places.append((index, side, start, count))
    where = jnp.stack([part[4] for part in parts]).astype(jnp.int32) * cell_rows
    smem = pl.BlockSpec(memory_space=pltpu.SMEM)
    return pl.pallas_call(
        functools.partial(square_kernel, tuple(places), cell_rows),
        out_shape=jax.ShapeDtypeStruct((2 * cell_rows, width, width), BF16),
        in_specs=[smem, smem] + [pl.BlockSpec(memory_space=pl.ANY)] * len(pieces),
        out_specs=pl.BlockSpec(memory_space=pltpu.VMEM),
        scratch_shapes=[
            pltpu.VMEM((cells * cell_rows, width, width), BF16),
            pltpu.VMEM((cells * 2 * cell_rows + 1, width, width), BF16),
            pltpu.SemaphoreType.DMA((len(places),)),
        ],
        cost_estimate=pl.CostEstimate(
            flops=4 * cells * cell_rows * width**3,
            transcendentals=0,
            bytes_accessed=2 * 3 * cells * cell_rows * width * width,
        ),
        name="square_sum",
    )(where, picks, *pieces)


def body(basis_values, potential, task_pairs, task_owner, task_slot, matrix_blocks, matrix_columns):
    x, yl, c, z, yh = (lax.axis_index(axis) for axis in ALL)
    cell_rows, width = matrix_blocks.shape[2], matrix_blocks.shape[3]
    row_count = lax.axis_size(ROW)
    device_count = row_count * lax.axis_size(COL)
    cells = 2 * lax.axis_size(COL)
    half = cell_rows
    own = matrix_blocks.reshape(2 * cell_rows, width, width)

    owners, slots = task_owner.reshape(-1), task_slot.reshape(-1)
    task_count = owners.shape[0]
    number = jnp.arange(task_count, dtype=jnp.int32)
    earlier = (owners[:, None] == owners[None, :]) & (number[None, :] < number[:, None])
    ranks = jnp.sum(earlier.astype(jnp.int32), axis=1)
    spots = jnp.arange(device_count, dtype=jnp.int32)
    named = owners[None, :] == spots[:, None]
    send_slots = [
        jnp.max(jnp.where(named & (ranks == rank)[None, :], slots[None, :], -1), axis=1)
        for rank in range(2)
    ]
    own_columns = matrix_columns.reshape(1, -1)
    numbers = jnp.concatenate(
        [
            send_slots[0][:, None],
            send_slots[1][:, None],
            jnp.broadcast_to(own_columns, (device_count, own_columns.shape[1])),
        ],
        axis=1,
    )

    y_both = lax.all_to_all(jnp.concatenate([own, own]), "yh", 0, 0, tiled=True)
    y_low = shift(own, "yl", 1)
    x_behind, x_ahead = shift(own, "x", 1), shift(own, "x", -1)
    z_behind, z_ahead = shift(own, "z", 1), shift(own, "z", -1)
    send0, send1 = pair_blocks(
        basis_values[0, 0], potential[0], task_pairs[0, 0], owners, ranks, device_count
    )

    x_behind, x_ahead, z_behind, z_ahead, y_low, send0, send1 = lax.optimization_barrier(
        (x_behind, x_ahead, z_behind, z_ahead, y_low, send0, send1)
    )
    z_far0, z_far1 = shift(z_behind[:half], "z", 1), shift(z_ahead[half:], "z", -1)
    x_behind2, x_ahead2 = shift(y_low, "x", 1), shift(y_low, "x", -1)

    z_far0, z_far1, y_both, numbers, x_behind3, x_ahead3 = lax.optimization_barrier(
        (z_far0, z_far1, y_both, numbers, x_behind, x_ahead)
    )
    y_high = lax.dynamic_slice_in_dim(y_both, (1 - yh) * 2 * cell_rows, 2 * cell_rows, 0)
    z_behind2, z_ahead2 = shift(y_high, "z", 1), shift(y_high, "z", -1)
    x_far0, x_far1 = shift(x_behind3[:half], "x", 1), shift(x_ahead3[half:], "x", -1)
    numbers = lax.all_to_all(numbers[:, None, :], ALL, 0, 0, tiled=True)[:, 0, :]

    x_behind2, x_ahead2, z_behind2, z_ahead2, x_far0, x_far1, numbers, own2, send0 = (
        lax.optimization_barrier(
            (x_behind2, x_ahead2, z_behind2, z_ahead2, x_far0, x_far1, numbers, own, send0)
        )
    )
    arrived0 = lax.all_to_all(send0, ALL, 0, 0, tiled=True)
    x_far2, x_far3 = shift(x_behind2[:half], "x", 1), shift(x_ahead2[half:], "x", -1)
    z_far2, z_far3 = shift(z_behind2[:half], "z", 1), shift(z_ahead2[half:], "z", -1)

    arrived0, x_far2, x_far3, z_far2, z_far3, send1 = lax.optimization_barrier(
        (arrived0, x_far2, x_far3, z_far2, z_far3, send1)
    )
    arrived1 = lax.all_to_all(send1, ALL, 0, 0, tiled=True)

    parts = []

    def left(value, start, count, ring, pair, cell):
        first = 2 * (((z + ring) % 4) * 2 + (yh + pair) % 2) + cell
        parts.append((0, value, start, count, first))

    def right(value, *pieces):
        other = shift(value, "c", 1)
        for start, count, ring, pair, cell in pieces:
            base = 2 * (((x + ring) % 4) * 2 + (yl + pair) % 2)
            parts.append((1, value, start, count, 2 * (base // 2 * 2 + c) + cell))
            parts.append((1, other, start, count, 2 * (base // 2 * 2 + 1 - c) + cell))

    left(own, 0, 2, 0, 0, 0)
    left(z_behind, 0, 2, 3, 0, 0)
    left(z_ahead, 0, 2, 1, 0, 0)
    left(y_high, 0, 2, 0, 1, 0)
    left(z_behind2, 0, 2, 3, 1, 0)
    left(z_ahead2, 0, 2, 1, 1, 0)
    left(z_far0, 0, 1, 2, 0, 0)
    left(z_far1, 0, 1, 2, 0, 1)
    left(z_far2, 0, 1, 2, 1, 0)
    left(z_far3, 0, 1, 2, 1, 1)
    right(own2, (0, 2, 0, 0, 0))
    right(x_behind, (0, 2, 3, 0, 0))
    right(x_ahead, (0, 2, 1, 0, 0))
    right(y_low, (0, 2, 0, 1, 0))
    right(x_behind2, (0, 2, 3, 1, 0))
    right(x_ahead2, (0, 2, 1, 1, 0))
    right(x_far0, (0, 1, 2, 0, 0))
    right(x_far1, (0, 1, 2, 0, 1))
    right(x_far2, (0, 1, 2, 1, 0))
    right(x_far3, (0, 1, 2, 1, 1))

    every = numbers[:, 2:].reshape(row_count, cells, cell_rows)
    me_row = (x * 2 + yl) * 2 + c
    me_col = z * 2 + yh
    left_columns = lax.dynamic_index_in_dim(every, me_row, 0, keepdims=False)
    right_columns = lax.dynamic_slice_in_dim(every, 2 * me_col, 2, 1)
    target = matrix_columns.reshape(2, cell_rows)
    slot_range = jnp.arange(cell_rows, dtype=jnp.int32)
    cell_range = jnp.arange(cells, dtype=jnp.int32)
    chosen = left_columns.T[:, :, None, None] == slot_range
    found = jnp.sum(jnp.where(chosen, right_columns[None], 0), axis=-1)
    spot = (cell_range[None, :, None] * 2 + jnp.arange(2, dtype=jnp.int32)) * cell_rows
    spot = spot + left_columns.T[:, :, None]
    picks = jnp.where(found == target.T[:, None, :], spot, cells * 2 * cell_rows)
    square = square_sum(picks.reshape(-1), parts, cells, cell_rows, width)

    partial = fock_sum(numbers[:, 0], [], arrived0, 2 * cell_rows, F32)
    fock = fock_sum(numbers[:, 1], [partial], arrived1, 2 * cell_rows, BF16)
    shape = (1, 2, cell_rows, width, width)
    return fock.reshape(shape), square.reshape(shape)


def solution(mesh):
    finer = Mesh(mesh.devices.reshape(4, 2, 2, 4, 2), ALL)
    return jax.shard_map(
        body,
        mesh=finer,
        in_specs=(
            P(ROW, COL, None, None, None),
            P(ROW, COL, None),
            P(ROW, COL, None, None),
            P(ROW, COL, None, None),
            P(ROW, COL, None),
            P(ROW, COL, None, None, None),
            P(ROW, COL, None),
        ),
        out_specs=(P(ROW, COL, None, None, None), P(ROW, COL, None, None, None)),
        check_vma=False,
    )
```

```python
import functools

import jax
import jax.numpy as jnp
from jax import lax
from jax.experimental import pallas as pl
from jax.experimental.pallas import tpu as pltpu
from jax.sharding import Mesh
from jax.sharding import PartitionSpec as P

ROW = ("x", "yl", "c")
COL = ("z", "yh")
ALL = ROW + COL
F32 = jnp.float32
BF16 = jnp.bfloat16


def shift(value, axis, step):
    size = lax.axis_size(axis)
    return lax.ppermute(value, axis, [(i, (i + step) % size) for i in range(size)])


def pair_kernel(pairs, owners, ranks, basis, potential, send0, send1, weighted, table, sem):
    local_count, width, points = basis.shape
    task_count = owners.shape[0]
    for a in range(local_count):
        weighted[a] = (basis[a].astype(F32) * potential[...]).astype(BF16)

    def columns(step, carry):
        left = weighted[...].reshape(local_count * width, points)
        right = basis[pl.ds(2 * step, 2)].reshape(2 * width, points)
        product = lax.dot_general(left, right, (((1,), (1,)), ((), ())), preferred_element_type=F32)
        product = product.astype(BF16).reshape(local_count, width, 2 * width)
        table[2 * step] = product[:, :, :width]
        table[2 * step + 1] = product[:, :, width:]
        return carry

    lax.fori_loop(0, local_count // 2, columns, 0)

    def start(t, carry):
        block = table.at[pairs[2 * t + 1], pairs[2 * t]]

        @pl.when(ranks[t] == 0)
        def _():
            pltpu.make_async_copy(block, send0.at[owners[t]], sem).start()

        @pl.when(ranks[t] != 0)
        def _():
            pltpu.make_async_copy(block, send1.at[owners[t]], sem).start()

        return carry

    lax.fori_loop(0, task_count, start, 0)
    whole = send0.at[pl.ds(0, task_count)]
    pltpu.make_async_copy(whole, whole, sem).wait()


def pair_blocks(basis, potential, pairs, owners, ranks, device_count):
    local_count, width, points = basis.shape
    task_count = owners.shape[0]
    smem = pl.BlockSpec(memory_space=pltpu.SMEM)
    vmem = pl.BlockSpec(memory_space=pltpu.VMEM)
    return pl.pallas_call(
        pair_kernel,
        out_shape=[jax.ShapeDtypeStruct((device_count, width, width), BF16)] * 2,
        in_specs=[smem, smem, smem, vmem, vmem],
        out_specs=[pl.BlockSpec(memory_space=pl.ANY)] * 2,
        scratch_shapes=[
            pltpu.VMEM((local_count, width, points), BF16),
            pltpu.VMEM((local_count, local_count, width, width), BF16),
            pltpu.SemaphoreType.DMA,
        ],
        cost_estimate=pl.CostEstimate(
            flops=2 * (local_count * width) ** 2 * points,
            transcendentals=0,
            bytes_accessed=2 * basis.size + 2 * task_count * width * width,
        ),
        name="pair_blocks",
    )(pairs.reshape(-1), owners, ranks, basis, potential)


def fock_kernel(order, starts, *refs):
    *before, arrived, out = refs

    def one_slot(slot, carry):
        if before:
            total = before[0][slot]
        else:
            total = jnp.zeros(out.shape[1:], F32)

        def add(p, total):
            return total + arrived[order[p]].astype(F32)

        total = lax.fori_loop(starts[slot], starts[slot + 1], add, total)
        out[slot] = total.astype(out.dtype)
        return carry

    lax.fori_loop(0, out.shape[0], one_slot, 0)


def fock_sum(slots, before, arrived, slot_count, kind):
    count, width, _ = arrived.shape
    number = jnp.arange(count, dtype=jnp.int32)
    valid = slots >= 0
    same = slots[None, :] == slots[:, None]
    ahead = (slots[None, :] < slots[:, None]) | (same & (number[None, :] < number[:, None]))
    spot = jnp.sum((ahead & valid[None, :]).astype(jnp.int32), axis=1)
    hit = (spot[None, :] == number[:, None]) & valid[None, :]
    order = jnp.sum(jnp.where(hit, number[None, :], 0), axis=1)
    bounds = jnp.arange(slot_count + 1, dtype=jnp.int32)
    starts = jnp.sum((valid & (slots < bounds[:, None])).astype(jnp.int32), axis=1)
    smem = pl.BlockSpec(memory_space=pltpu.SMEM)
    vmem = pl.BlockSpec(memory_space=pltpu.VMEM)
    return pl.pallas_call(
        fock_kernel,
        out_shape=jax.ShapeDtypeStruct((slot_count, width, width), kind),
        in_specs=[smem, smem] + [vmem] * (len(before) + 1),
        out_specs=vmem,
        cost_estimate=pl.CostEstimate(
            flops=arrived.size, transcendentals=0, bytes_accessed=2 * arrived.size
        ),
        name="fock_sum",
    )(order, starts, *before, arrived)


def square_kernel(places, cell_rows, where, picks, *refs):
    *pieces, out, left, right, sems = refs
    cells = left.shape[0] // cell_rows
    width = left.shape[-1]
    zero = right.shape[0] - 1
    copies = []
    for n, (piece, side, start, count) in enumerate(places):
        source = pieces[piece].at[pl.ds(start * cell_rows, count * cell_rows)]
        first = pl.multiple_of(where[n], cell_rows)
        target = (left if side == 0 else right).at[pl.ds(first, count * cell_rows)]
        copies.append(pltpu.make_async_copy(source, target, sems.at[n]))
    for copy in copies:
        copy.start()
    right[zero] = jnp.zeros((width, width), BF16)
    for copy in copies:
        copy.wait()

    def block_row(q, carry):
        total = jnp.zeros((width, 2 * width), F32)
        for k in range(0, cells, 2):
            a = jnp.concatenate([left[k * cell_rows + q], left[(k + 1) * cell_rows + q]], axis=1)
            b = [[right[picks[(q * cells + k + h) * 2 + j]] for j in range(2)] for h in range(2)]
            b = jnp.concatenate([jnp.concatenate(b[h], axis=1) for h in range(2)], axis=0)
            total += jnp.dot(a, b, preferred_element_type=F32)
        out[q] = total[:, :width].astype(BF16)
        out[cell_rows + q] = total[:, width:].astype(BF16)
        return carry

    lax.fori_loop(0, cell_rows, block_row, 0)


def square_sum(picks, parts, cells, cell_rows, width):
    pieces = []
    places = []
    for side, value, start, count, first in parts:
        if not any(value is piece for piece in pieces):
            pieces.append(value)
        index = [value is piece for piece in pieces].index(True)
        places.append((index, side, start, count))
    where = jnp.stack([part[4] for part in parts]).astype(jnp.int32) * cell_rows
    smem = pl.BlockSpec(memory_space=pltpu.SMEM)
    return pl.pallas_call(
        functools.partial(square_kernel, tuple(places), cell_rows),
        out_shape=jax.ShapeDtypeStruct((2 * cell_rows, width, width), BF16),
        in_specs=[smem, smem] + [pl.BlockSpec(memory_space=pl.ANY)] * len(pieces),
        out_specs=pl.BlockSpec(memory_space=pltpu.VMEM),
        scratch_shapes=[
            pltpu.VMEM((cells * cell_rows, width, width), BF16),
            pltpu.VMEM((cells * 2 * cell_rows + 1, width, width), BF16),
            pltpu.SemaphoreType.DMA((len(places),)),
        ],
        cost_estimate=pl.CostEstimate(
            flops=4 * cells * cell_rows * width**3,
            transcendentals=0,
            bytes_accessed=2 * 3 * cells * cell_rows * width * width,
        ),
        name="square_sum",
    )(where, picks, *pieces)


def body(basis_values, potential, task_pairs, task_owner, task_slot, matrix_blocks, matrix_columns):
    x, yl, c, z, yh = (lax.axis_index(axis) for axis in ALL)
    cell_rows, width = matrix_blocks.shape[2], matrix_blocks.shape[3]
    row_count = lax.axis_size(ROW)
    device_count = row_count * lax.axis_size(COL)
    cells = 2 * lax.axis_size(COL)
    half = cell_rows
    own = matrix_blocks.reshape(2 * cell_rows, width, width)

    owners, slots = task_owner.reshape(-1), task_slot.reshape(-1)
    task_count = owners.shape[0]
    number = jnp.arange(task_count, dtype=jnp.int32)
    earlier = (owners[:, None] == owners[None, :]) & (number[None, :] < number[:, None])
    ranks = jnp.sum(earlier.astype(jnp.int32), axis=1)
    spots = jnp.arange(device_count, dtype=jnp.int32)
    named = owners[None, :] == spots[:, None]
    send_slots = [
        jnp.max(jnp.where(named & (ranks == rank)[None, :], slots[None, :], -1), axis=1)
        for rank in range(2)
    ]
    own_columns = matrix_columns.reshape(1, -1)
    numbers = jnp.concatenate(
        [
            send_slots[0][:, None],
            send_slots[1][:, None],
            jnp.broadcast_to(own_columns, (device_count, own_columns.shape[1])),
        ],
        axis=1,
    )

    y_both = lax.all_to_all(jnp.concatenate([own, own]), "yh", 0, 0, tiled=True)
    y_low = shift(own, "yl", 1)
    x_behind, x_ahead = shift(own, "x", 1), shift(own, "x", -1)
    z_behind, z_ahead = shift(own, "z", 1), shift(own, "z", -1)

    x_behind, x_ahead, z_behind, z_ahead, y_low, basis = lax.optimization_barrier(
        (x_behind, x_ahead, z_behind, z_ahead, y_low, basis_values)
    )
    z_far0, z_far1 = shift(z_behind[:half], "z", 1), shift(z_ahead[half:], "z", -1)
    x_behind2, x_ahead2 = shift(y_low, "x", 1), shift(y_low, "x", -1)

    send0, send1 = pair_blocks(
        basis[0, 0], potential[0], task_pairs[0, 0], owners, ranks, device_count
    )

    z_far0, z_far1, y_both, numbers, x_behind3, x_ahead3, send0, send1 = lax.optimization_barrier(
        (z_far0, z_far1, y_both, numbers, x_behind, x_ahead, send0, send1)
    )
    y_high = lax.dynamic_slice_in_dim(y_both, (1 - yh) * 2 * cell_rows, 2 * cell_rows, 0)
    z_behind2, z_ahead2 = shift(y_high, "z", 1), shift(y_high, "z", -1)
    x_far0, x_far1 = shift(x_behind3[:half], "x", 1), shift(x_ahead3[half:], "x", -1)
    numbers = lax.all_to_all(numbers[:, None, :], ALL, 0, 0, tiled=True)[:, 0, :]

    x_behind2, x_ahead2, z_behind2, z_ahead2, x_far0, x_far1, numbers, own2, send0 = (
        lax.optimization_barrier(
            (x_behind2, x_ahead2, z_behind2, z_ahead2, x_far0, x_far1, numbers, own, send0)
        )
    )
    arrived0 = lax.all_to_all(send0, ALL, 0, 0, tiled=True)
    x_far2, x_far3 = shift(x_behind2[:half], "x", 1), shift(x_ahead2[half:], "x", -1)
    z_far2, z_far3 = shift(z_behind2[:half], "z", 1), shift(z_ahead2[half:], "z", -1)

    arrived0, x_far2, x_far3, z_far2, z_far3, send1 = lax.optimization_barrier(
        (arrived0, x_far2, x_far3, z_far2, z_far3, send1)
    )
    arrived1 = lax.all_to_all(send1, ALL, 0, 0, tiled=True)

    parts = []

    def left(value, start, count, ring, pair, cell):
        first = 2 * (((z + ring) % 4) * 2 + (yh + pair) % 2) + cell
        parts.append((0, value, start, count, first))

    def right(value, *pieces):
        other = shift(value, "c", 1)
        for start, count, ring, pair, cell in pieces:
            base = 2 * (((x + ring) % 4) * 2 + (yl + pair) % 2)
            parts.append((1, value, start, count, 2 * (base // 2 * 2 + c) + cell))
            parts.append((1, other, start, count, 2 * (base // 2 * 2 + 1 - c) + cell))

    left(own, 0, 2, 0, 0, 0)
    left(z_behind, 0, 2, 3, 0, 0)
    left(z_ahead, 0, 2, 1, 0, 0)
    left(y_high, 0, 2, 0, 1, 0)
    left(z_behind2, 0, 2, 3, 1, 0)
    left(z_ahead2, 0, 2, 1, 1, 0)
    left(z_far0, 0, 1, 2, 0, 0)
    left(z_far1, 0, 1, 2, 0, 1)
    left(z_far2, 0, 1, 2, 1, 0)
    left(z_far3, 0, 1, 2, 1, 1)
    right(own2, (0, 2, 0, 0, 0))
    right(x_behind, (0, 2, 3, 0, 0))
    right(x_ahead, (0, 2, 1, 0, 0))
    right(y_low, (0, 2, 0, 1, 0))
    right(x_behind2, (0, 2, 3, 1, 0))
    right(x_ahead2, (0, 2, 1, 1, 0))
    right(x_far0, (0, 1, 2, 0, 0))
    right(x_far1, (0, 1, 2, 0, 1))
    right(x_far2, (0, 1, 2, 1, 0))
    right(x_far3, (0, 1, 2, 1, 1))

    every = numbers[:, 2:].reshape(row_count, cells, cell_rows)
    me_row = (x * 2 + yl) * 2 + c
    me_col = z * 2 + yh
    left_columns = lax.dynamic_index_in_dim(every, me_row, 0, keepdims=False)
    right_columns = lax.dynamic_slice_in_dim(every, 2 * me_col, 2, 1)
    target = matrix_columns.reshape(2, cell_rows)
    slot_range = jnp.arange(cell_rows, dtype=jnp.int32)
    cell_range = jnp.arange(cells, dtype=jnp.int32)
    chosen = left_columns.T[:, :, None, None] == slot_range
    found = jnp.sum(jnp.where(chosen, right_columns[None], 0), axis=-1)
    spot = (cell_range[None, :, None] * 2 + jnp.arange(2, dtype=jnp.int32)) * cell_rows
    spot = spot + left_columns.T[:, :, None]
    picks = jnp.where(found == target.T[:, None, :], spot, cells * 2 * cell_rows)
    square = square_sum(picks.reshape(-1), parts, cells, cell_rows, width)

    partial = fock_sum(numbers[:, 0], [], arrived0, 2 * cell_rows, F32)
    fock = fock_sum(numbers[:, 1], [partial], arrived1, 2 * cell_rows, BF16)
    shape = (1, 2, cell_rows, width, width)
    return fock.reshape(shape), square.reshape(shape)


def solution(mesh):
    finer = Mesh(mesh.devices.reshape(4, 2, 2, 4, 2), ALL)
    return jax.shard_map(
        body,
        mesh=finer,
        in_specs=(
            P(ROW, COL, None, None, None),
            P(ROW, COL, None),
            P(ROW, COL, None, None),
            P(ROW, COL, None, None),
            P(ROW, COL, None),
            P(ROW, COL, None, None, None),
            P(ROW, COL, None),
        ),
        out_specs=(P(ROW, COL, None, None, None), P(ROW, COL, None, None, None)),
        check_vma=False,
    )
```
